32 devices in a mesh: row: 2 (over core), blk: 16 (over z, y, x).
Axes of the slice: x: 2, y: 2, z: 4, core: 2. Of those that a mesh axis runs over, the one named last changes fastest.
Arguments:
- state: float32 [2, 9, 5, 16, 2048], P('row', None, None, None, 'blk'), may hold values from -6 to 6
- inflow: float32 [9, 5, 2048], P(None, None, 'blk'), may hold values from -6 to 6
- blade_counts: int32 [2], replicated, may hold values from 20 to 60
- modes: int32 [1, 4], replicated, may hold values from 1 to 40
Outputs:
- advanced: float32 [2, 9, 5, 16, 2048], P('row', None, None, None, 'blk')
The draws below stay inside these ranges and needn't reach their ends.
All inputs are finite; a program needn't handle non-finite values.
Results may differ from the reference program's by a relative error of at most 0.0001.
Values sent between devices are 32-bit elements; how exact they have to be, the bound alone decides.
A program may use at most 64 MiB of HBM per device.

```python
import math
import jax
import jax.numpy as jnp
from jax import lax

VARS = 5
HARM = 4
CJ = 16
CT = 128
ROWS = 2
IFACES = 1
NT = 2048
N_BLK = 16


def with_ends(values, stream_key, least, high):
    longest = values.shape.index(max(values.shape))
    spots = []
    for shift in (0, 1):
        where = [jax.random.randint(jax.random.fold_in(stream_key, axis), (), 0, length) for axis, length in enumerate(values.shape)]
        where[longest] = (where[longest] + shift) % values.shape[longest]
        spots.append(tuple(where))
    return values.at[spots[0]].set(least).at[spots[1]].set(high)


def block_scale(stream_key, extent, cuts, least, high):
    factor_of, own = 1.0, jax.random.fold_in(stream_key, 6)
    for axis_at, blocks in cuts:
        heights = jnp.exp(jax.random.uniform(jax.random.fold_in(own, axis_at), (blocks,), jnp.float32, least / len(cuts), high / len(cuts)))
        factor_of = factor_of * jnp.repeat(heights, extent[axis_at] // blocks).reshape([-1 if axis == axis_at else 1 for axis in range(len(extent))])
    return factor_of


def normal_values(own_key, extent, deviation, bound, shards=(), held_as=jnp.bfloat16):
    result = deviation * jax.random.normal(own_key, extent, jnp.float32)
    if shards:
        result = result * block_scale(own_key, extent, shards, -0.22, 0.18)
    return jnp.clip(result, -bound, bound).astype(held_as)


def setup_inputs(seed: int = 0) -> dict:
    key_of = jax.random.split(jax.random.key(seed), 5)
    state = normal_values(key_of[0], (ROWS, 2 * HARM + 1, VARS, CJ, NT), 1.0, 6.0, ((0, 2), (4, 16)), jnp.float32)
    inflow = normal_values(key_of[1], (2 * HARM + 1, VARS, NT), 1.0, 6.0, ((2, 16),), jnp.float32)
    blade_counts = jax.random.randint(key_of[2], (ROWS,), 20, 61).astype(jnp.int32)
    modes = with_ends(jax.random.randint(key_of[3], (IFACES, HARM), 1, 41), jax.random.fold_in(key_of[3], 1), 1, 40).astype(jnp.int32)
    return dict(state=state, inflow=inflow, blade_counts=blade_counts, modes=modes)


DIFFUSE = 0.05
FOURTH_SMOOTH = 0.03
COURANT = 0.6
FREQ_SCALE = 0.02
SECTION_WEIGHTS = (0.5, 1.0)


def residual(padded, frequency):
    inner_depth = padded.shape[2] - 4
    inner_width = padded.shape[3] - 4

    def window_at(source, shift_j, shift_t):
        return source[:, :, 2 + shift_j:2 + shift_j + inner_depth, 2 + shift_t:2 + shift_t + inner_width]

    steady = padded[0]
    speed_axial = 1.0 + 0.5 * jnp.tanh(steady[1])
    speed_turn = 0.5 * jnp.tanh(steady[2])
    cosines = padded[1::2]
    sines = padded[2::2]
    stress = 0.5 * jnp.sum(cosines[:, 1:2] * cosines + sines[:, 1:2] * sines, axis=0)
    flux_axial = speed_axial * padded + jnp.concatenate([stress[None], jnp.zeros_like(padded[1:])], axis=0)
    flux_turn = speed_turn * padded
    center = window_at(padded, 0, 0)
    neighbours = window_at(padded, 1, 0) + window_at(padded, -1, 0) + window_at(padded, 0, 1) + window_at(padded, 0, -1)
    farther = window_at(padded, 2, 0) + window_at(padded, -2, 0) + window_at(padded, 0, 2) + window_at(padded, 0, -2)
    convect = -0.5 * (window_at(flux_axial, 1, 0) - window_at(flux_axial, -1, 0)) - 0.5 * (window_at(flux_turn, 0, 1) - window_at(flux_turn, 0, -1))
    second = neighbours - 4.0 * center
    fourth = farther - 4.0 * neighbours + 12.0 * center
    rates = frequency[:, None, None, None]
    source_real = rates * center[2::2]
    source_imag = -rates * center[1::2]
    paired = jnp.stack([source_real, source_imag], axis=1).reshape((-1,) + center.shape[1:])
    source = jnp.concatenate([jnp.zeros_like(center[0:1]), paired], axis=0)
    return convect + DIFFUSE * second - FOURTH_SMOOTH * fourth + source


def local_step(field):
    steady = field[0]
    return COURANT / (1.0 + 0.5 * jnp.tanh(steady[1]) + jnp.abs(0.5 * jnp.tanh(steady[2])))


def rotate_modes(planes, table, sign, columns, total):
    pieces = [planes[0]]
    for harmonic in range(planes.shape[0] // 2):
        turns = jnp.remainder(table[harmonic] * columns, total)
        angle = (2.0 * math.pi / total) * turns.astype(jnp.float32)
        cosine = jnp.cos(angle)
        sine = sign * jnp.sin(angle)
        real_part = planes[1 + 2 * harmonic]
        imag_part = planes[2 + 2 * harmonic]
        pieces.append(real_part * cosine - imag_part * sine)
        pieces.append(real_part * sine + imag_part * cosine)
    return jnp.stack(pieces)


def pad_columns(planes):
    return jnp.pad(planes, ((0, 0), (0, 0), (0, 0), (2, 2)))


def reference(state, inflow, blade_counts, modes):
    columns = jnp.arange(NT, dtype=jnp.int32)
    orders = jnp.arange(1, HARM + 1, dtype=jnp.float32)

    def row_residual(current, row_number, frequency):
        core = current[row_number]
        if row_number == 0:
            lower = jnp.concatenate([inflow[:, :, None, :], inflow[:, :, None, :]], axis=2)
        else:
            lower = rotate_modes(current[row_number - 1][:, :, CJ - 2:], modes[row_number - 1], 1.0, columns, NT)
        if row_number == ROWS - 1:
            last_plane = core[:, :, CJ - 1:]
            upper = jnp.concatenate([last_plane, last_plane], axis=2)
        else:
            upper = rotate_modes(current[row_number + 1][:, :, :2], modes[row_number], -1.0, columns, NT)
        wrapped = jnp.concatenate([core[..., NT - 2:], core, core[..., :2]], axis=3)
        padded = jnp.concatenate([pad_columns(lower), wrapped, pad_columns(upper)], axis=2)

        def block_residual(block_number):
            piece = lax.dynamic_slice_in_dim(padded, block_number * CT, CT + 4, 3)
            return residual(piece, frequency)

        blocks = lax.map(block_residual, jnp.arange(N_BLK, dtype=jnp.int32))
        return jnp.moveaxis(blocks, 0, 3).reshape((2 * HARM + 1, VARS, CJ, NT))

    step_sizes = [local_step(state[row_number]) for row_number in range(ROWS)]
    frequencies = [FREQ_SCALE * blade_counts[row_number].astype(jnp.float32) * orders for row_number in range(ROWS)]
    current = state
    for weight in SECTION_WEIGHTS:
        current = jnp.stack([state[row_number] + weight * step_sizes[row_number] * row_residual(current, row_number, frequencies[row_number]) for row_number in range(ROWS)])
    return current
```

```python
import functools
import math

import jax
import jax.numpy as jnp
from jax import lax
from jax.experimental import pallas as pl
from jax.experimental.pallas import tpu as pltpu
from jax.sharding import PartitionSpec as P

DIFFUSE = 0.05
FOURTH_SMOOTH = 0.03
COURANT = 0.6
FREQ_SCALE = 0.02
MESH = pl.DeviceIdType.MESH
NEAR = DIFFUSE + 4.0 * FOURTH_SMOOTH
CENTER = -4.0 * DIFFUSE - 12.0 * FOURTH_SMOOTH
HALO = 4
PAD = 8
BATCH = 6
PIECES = 3


def packing(items, layers, width):
    seg = width // (layers + 2)
    slots = width // (layers * seg) * (seg // HALO)
    return seg, -(-items // slots)


def section(src, base, rows, start, start_base, weight, rates, emit, comps, nvars):
    width = src.shape[2]

    def at(c, v, off):
        return src[c * nvars + v, base + off : base + off + rows, :]

    def opening(v):
        return start[v, start_base : start_base + rows, :]

    coef_up = (NEAR - 0.5) - 0.25 * jnp.tanh(at(0, 1, 1))
    coef_down = (NEAR + 0.5) + 0.25 * jnp.tanh(at(0, 1, -1))
    half_turn = 0.25 * jnp.tanh(at(0, 2, 0))
    coef_next = NEAR - pltpu.roll(half_turn, width - 1, 1)
    coef_prev = NEAR + pltpu.roll(half_turn, 1, 1)
    step = (weight * COURANT) / (
        1.0 + 0.5 * jnp.tanh(opening(1)) + jnp.abs(0.5 * jnp.tanh(opening(2)))
    )

    def one(c, v):
        here, up, down = at(c, v, 0), at(c, v, 1), at(c, v, -1)
        far = (
            at(c, v, 2)
            + at(c, v, -2)
            + pltpu.roll(here, width - 2, 1)
            + pltpu.roll(here, 2, 1)
        )
        total = (
            coef_up * up
            + coef_down * down
            + coef_next * pltpu.roll(here, width - 1, 1)
            + coef_prev * pltpu.roll(here, 1, 1)
            + CENTER * here
            - FOURTH_SMOOTH * far
        )
        return here, up, down, total

    def put(c, v, total):
        k = c * nvars + v
        emit(k, start[k, start_base : start_base + rows, :] + step * total)

    def per_var(v, carry):
        stress = None
        for n in range(1, comps // 2 + 1):
            real, real_up, real_down, real_total = one(2 * n - 1, v)
            imag, imag_up, imag_down, imag_total = one(2 * n, v)
            rate = rates[n - 1]
            put(2 * n - 1, v, real_total + rate * imag)
            put(2 * n, v, imag_total - rate * real)
            term = (
                at(2 * n - 1, 1, 1) * real_up
                + at(2 * n, 1, 1) * imag_up
                - at(2 * n - 1, 1, -1) * real_down
                - at(2 * n, 1, -1) * imag_down
            )
            stress = term if stress is None else stress + term
        _, _, _, total = one(0, v)
        put(0, v, total - 0.25 * stress)
        return carry

    lax.fori_loop(0, nvars, per_var, 0, unroll=True)


def kernel(
    rows_total,
    blocks,
    nvars,
    modes_in,
    counts_in,
    state,
    inflow,
    out,
    e_main,
    e_edge,
    f_main,
    f_edge,
    x_main,
    y_main,
    in_main,
    in_edge,
    pack,
    corner,
    halo,
    low,
    high,
    low_halo,
    high_halo,
    modes,
    counts,
    local_sem,
    send_sem,
    recv_sem,
):
    fields, depth, width = state.shape
    comps = fields // nvars
    harmonics = comps // 2
    layers = depth // 8
    seg, groups = packing(fields + comps, layers, width)
    per = seg // HALO
    slots = width // (layers * seg) * per
    total_columns = width * blocks
    row = lax.axis_index("row")
    blk = lax.axis_index("blk")
    right = lax.rem(blk + 1, blocks)
    left = lax.rem(blk + blocks - 1, blocks)
    has_low = row > 0
    has_high = row < rows_total - 1

    barrier = pltpu.get_barrier_semaphore()

    def greet(r, b):
        pl.semaphore_signal(barrier, inc=1, device_id={"row": r, "blk": b}, device_id_type=MESH)

    greet(row, right)
    greet(row, left)

    @pl.when(has_high)
    def _():
        greet(row + 1, right)
        greet(row + 1, left)
        greet(row + 1, blk)

    @pl.when(has_low)
    def _():
        greet(row - 1, right)
        greet(row - 1, left)
        greet(row - 1, blk)

    def fetch(first, last, index):
        return pltpu.make_async_copy(
            state.at[first:last], e_main.at[first:last, PAD : PAD + depth, :], local_sem.at[index]
        )

    bounds = [(g * slots, min((g + 1) * slots, fields)) for g in range(groups) if g * slots < fields]
    for index, (opening, closing) in enumerate(bounds):
        piece = -(-(closing - opening) // PIECES)
        for first in range(opening, closing, piece):
            fetch(first, min(first + piece, closing), index).start()
    count = len(bounds)
    fetch_in = pltpu.make_async_copy(inflow, in_main, local_sem.at[count])
    fetch_modes = pltpu.make_async_copy(modes_in, modes, local_sem.at[count + 1])
    fetch_counts = pltpu.make_async_copy(counts_in, counts, local_sem.at[count + 2])
    for copy in (fetch_in, fetch_modes, fetch_counts):
        copy.start()

    shape = (8, width)
    sub = lax.broadcasted_iota(jnp.int32, shape, 0)
    lane = lax.broadcasted_iota(jnp.int32, shape, 1)
    part, off = lane // seg, lane % seg
    def shifted(value, by):
        return pltpu.roll(value, by % width, 1)

    def spot_of(item):
        g, m = item // slots, item % slots
        return g, (m % per) * HALO + (m // per) * layers * seg

    for g in range(groups):
        if g < count:
            fetch(*bounds[g], g).wait()
        edges = [jnp.zeros(shape, jnp.float32), jnp.zeros(shape, jnp.float32)]
        for k in range(g * slots, min((g + 1) * slots, fields)):
            _, p = spot_of(k)
            for layer in range(layers):
                q = p + layer * seg
                value = e_main[k, PAD + 8 * layer : PAD + 8 * layer + 8, :]
                spot = lane // HALO == q // HALO
                edges[0] = jnp.where(spot, shifted(value, q), edges[0])
                edges[1] = jnp.where(spot, shifted(value, q + HALO), edges[1])
        pack[0, g] = edges[0]
        pack[1, g] = edges[1]
    fetch_in.wait()
    lane_in = lax.broadcasted_iota(jnp.int32, (nvars, width), 1)
    for c in range(comps):
        g, p = spot_of(fields + c)
        spot = lane_in // HALO == p // HALO
        value = in_main[c]
        pack[0, g, 0:nvars, :] = jnp.where(spot, shifted(value, p), pack[0, g, 0:nvars, :])
        pack[1, g, 0:nvars, :] = jnp.where(spot, shifted(value, p + HALO), pack[1, g, 0:nvars, :])
    for side in range(2):
        for g in range(groups):
            corner[0, side, 2 * g : 2 * g + 2, :] = pack[side, g, 0:2, :]
            corner[1, side, 2 * g : 2 * g + 2, :] = pack[side, g, 6:8, :]

    greeters = 2 + 3 * has_low.astype(jnp.int32) + 3 * has_high.astype(jnp.int32)
    pl.semaphore_wait(barrier, greeters)

    def send(src, dst, index, r, b):
        return pltpu.make_async_remote_copy(
            src_ref=src,
            dst_ref=dst,
            send_sem=send_sem.at[0],
            recv_sem=recv_sem.at[index],
            device_id={"row": r, "blk": b},
            device_id_type=MESH,
        )

    level = [send(pack.at[1], halo.at[0], 0, row, right), send(pack.at[0], halo.at[1], 1, row, left)]
    up = [
        send(corner.at[1, 1], low_halo.at[0], 2, row + 1, right),
        send(corner.at[1, 0], low_halo.at[1], 3, row + 1, left),
        send(state.at[:, pl.ds(depth - 8, 8), :], low, 4, row + 1, blk),
    ]
    down = [
        send(corner.at[0, 1], high_halo.at[0], 5, row - 1, right),
        send(corner.at[0, 0], high_halo.at[1], 6, row - 1, left),
        send(state.at[:, pl.ds(0, 8), :], high, 7, row - 1, blk),
    ]
    for copy in level:
        copy.start()

    @pl.when(has_high)
    def _():
        for copy in up:
            copy.start()

    @pl.when(has_low)
    def _():
        for copy in down:
            copy.start()

    def place(value, where_to):
        at_off = lax.broadcasted_iota(jnp.int32, value.shape, 1) % seg
        start = where_to * seg
        return jnp.where(
            at_off < 3 * HALO,
            shifted(value, start + HALO),
            shifted(value, start + 5 * HALO - width),
        )

    for k in range(fields):
        value = jnp.zeros(shape, jnp.float32)
        for layer in range(layers):
            plane = e_main[k, PAD + 8 * layer : PAD + 8 * layer + 8, :]
            value = jnp.where(part == layer + 1, place(plane, layer + 1), value)
        e_edge[k, 2:10, :] = value
    for c in range(comps):
        in_edge[c] = place(in_main[c], 1)

    fetch_modes.wait()
    fetch_counts.wait()
    sign = jnp.where((sub // 2) % 2 == 0, 1.0, -1.0).astype(jnp.float32)

    def mode_of(interface, n):
        value = jnp.int32(0)
        for i in range(rows_total - 1):
            value = value + jnp.where(interface == i, modes[i, n], 0)
        return value

    def count_of(wanted):
        value = jnp.int32(0)
        for i in range(rows_total):
            value = value + jnp.where(wanted == i, counts[i], 0)
        return value.astype(jnp.float32)

    def tables(modes_at, columns):
        made = []
        for n in range(harmonics):
            product = modes_at(n) * columns
            if total_columns & (total_columns - 1) == 0:
                turns = product & (total_columns - 1)
            else:
                turns = jnp.remainder(product, total_columns)
            angle = (2.0 * math.pi / total_columns) * turns.astype(jnp.float32)
            made.append((jnp.cos(angle), jnp.sin(angle)))
        return made

    tab_main = [
        (cosine, sign * sine)
        for cosine, sine in tables(
            lambda n: jnp.where(sub < 4, mode_of(row - 1, n), mode_of(row, n)), blk * width + lane
        )
    ]
    edge_column = jnp.where(off < 3 * HALO, off - HALO, off + width - 5 * HALO)

    def edge_mode(n):
        lower, upper = mode_of(row - 1, n), mode_of(row, n)
        rising = jnp.where(part == 0, lower, jnp.where(part == layers, upper, 0))
        falling = jnp.where(part == 1, -lower, jnp.where(part == layers + 1, -upper, 0))
        return jnp.where(sub < 4, falling, rising)

    tab_edge = tables(edge_mode, blk * width + edge_column)
    own_rate = FREQ_SCALE * count_of(row)
    next_rate = jnp.where(sub < 4, FREQ_SCALE * count_of(row - 1), FREQ_SCALE * count_of(row + 1))
    own_rates = [own_rate * float(n) for n in range(1, harmonics + 1)]
    edge_rate = jnp.where(
        part == 0,
        FREQ_SCALE * count_of(row - 1),
        jnp.where(part == layers + 1, FREQ_SCALE * count_of(row + 1), own_rate),
    )
    edge_rates = [edge_rate * float(n) for n in range(1, harmonics + 1)]
    next_rates = [next_rate * float(n) for n in range(1, harmonics + 1)]

    @pl.when(has_low)
    def _():
        up[2].wait_recv()
        x_main[:, 0:4, :] = low[:, 4:8, :]
        for k in range(fields):
            e_edge[k, 2:10, :] = jnp.where(part == 0, place(low[k], 0), e_edge[k, 2:10, :])

    @pl.when(jnp.logical_not(has_low))
    def _():
        x_main[:, 0:4, :] = jnp.zeros((fields, 4, width), jnp.float32)

    @pl.when(has_high)
    def _():
        down[2].wait_recv()
        x_main[:, 8:12, :] = high[:, 0:4, :]
        for k in range(fields):
            e_edge[k, 2:10, :] = jnp.where(
                part == layers + 1, place(high[k], layers + 1), e_edge[k, 2:10, :]
            )

    @pl.when(jnp.logical_not(has_high))
    def _():
        x_main[:, 8:12, :] = jnp.zeros((fields, 4, width), jnp.float32)

    def ends(field, inflow_of):
        @pl.when(jnp.logical_not(has_low))
        def _():
            for c in range(comps):
                for v in range(nvars):
                    plane = inflow_of[c, v : v + 1, :]
                    field[c * nvars + v, PAD - 2 : PAD, :] = jnp.broadcast_to(plane, (2, width))

        @pl.when(jnp.logical_not(has_high))
        def _():
            for k in range(fields):
                plane = field[k, PAD + depth - 1 : PAD + depth, :]
                field[k, PAD + depth : PAD + depth + 2, :] = jnp.broadcast_to(plane, (2, width))

    def turn(load, save, table):
        def per_var(v, carry):
            save(v, load(v))
            for n in range(harmonics):
                cosine, sine = table[n]
                real_at, imag_at = (2 * n + 1) * nvars + v, (2 * n + 2) * nvars + v
                real, imag = load(real_at), load(imag_at)
                save(real_at, real * cosine - imag * sine)
                save(imag_at, real * sine + imag * cosine)
            return carry

        lax.fori_loop(0, nvars, per_var, 0, unroll=True)

    def both(e, f, x, y, inflow_of, table, emit):
        x[:, 4:6, :] = e[:, PAD : PAD + 2, :]
        x[:, 6:8, :] = e[:, PAD + depth - 2 : PAD + depth, :]

        def save_first(k, value):
            e[k, PAD - 2 : PAD, :] = value[0:2]
            x[k, 4:8, :] = value[2:6]
            e[k, PAD + depth : PAD + depth + 2, :] = value[6:8]

        turn(lambda k: x[k, 2:10, :], save_first, table)
        ends(e, inflow_of)

        def keep_y(k, value):
            y[k] = value

        def keep_f(k, value):
            f[k, PAD : PAD + depth, :] = value

        section(x, 2, 8, x, 2, 0.5, next_rates, keep_y, comps, nvars)
        section(e, PAD, depth, e, PAD, 0.5, own_rates, keep_f, comps, nvars)

        def save_second(k, value):
            f[k, PAD - 2 : PAD, :] = value[0:2]
            f[k, PAD + depth : PAD + depth + 2, :] = value[6:8]

        turn(lambda k: y[k], save_second, table)
        ends(f, inflow_of)
        section(f, PAD, depth, e, PAD, 1.0, own_rates, emit, comps, nvars)

    def emit_main(k, value):
        out[k] = value

    both(e_main, f_main, x_main, y_main, in_main, tab_main, emit_main)

    for copy in level:
        copy.wait_recv()

    def beyond(value, from_left, from_right, p, start, first, last):
        at_lane = lax.broadcasted_iota(jnp.int32, value.shape, 1)
        at_part, at_off = at_lane // seg, at_lane % seg
        here = jnp.logical_and(at_part >= first, at_part <= last)
        in_left = jnp.logical_and(here, at_off < HALO)
        in_right = jnp.logical_and(here, at_off >= 5 * HALO)
        left_part = shifted(from_left, start - p)
        right_part = shifted(from_right, start + 5 * HALO - p)
        return jnp.where(in_left, left_part, jnp.where(in_right, right_part, value))

    for k in range(fields):
        g, p = spot_of(k)
        e_edge[k, 2:10, :] = beyond(
            e_edge[k, 2:10, :], halo[0, g], halo[1, g], p, seg, 1, layers
        )

    @pl.when(has_low)
    def _():
        up[0].wait_recv()
        up[1].wait_recv()
        for k in range(fields):
            g, p = spot_of(k)
            spot = slice(2 * g, 2 * g + 2)
            e_edge[k, 8:10, :] = beyond(
                e_edge[k, 8:10, :],
                low_halo[0, spot, :],
                low_halo[1, spot, :],
                p + (layers - 1) * seg,
                0,
                0,
                0,
            )

    @pl.when(jnp.logical_not(has_low))
    def _():
        for c in range(comps):
            g, p = spot_of(fields + c)
            in_edge[c] = beyond(
                in_edge[c], halo[0, g, 0:nvars, :], halo[1, g, 0:nvars, :], p, seg, 1, 1
            )

    @pl.when(has_high)
    def _():
        down[0].wait_recv()
        down[1].wait_recv()
        for k in range(fields):
            g, p = spot_of(k)
            spot = slice(2 * g, 2 * g + 2)
            e_edge[k, 2:4, :] = beyond(
                e_edge[k, 2:4, :],
                high_halo[0, spot, :],
                high_halo[1, spot, :],
                p,
                (layers + 1) * seg,
                layers + 1,
                layers + 1,
            )

    def link(field):
        def save(k, value):
            field[k, 0:2, :] = shifted(value, seg)[6:8]
            field[k, 10:12, :] = shifted(value, -seg)[0:2]

        turn(lambda k: field[k, 2:10, :], save, tab_edge)
        two = lax.broadcasted_iota(jnp.int32, (2, width), 1) // seg

        @pl.when(jnp.logical_not(has_low))
        def _():
            for c in range(comps):
                for v in range(nvars):
                    k = c * nvars + v
                    plane = jnp.broadcast_to(in_edge[c, v : v + 1, :], (2, width))
                    field[k, 0:2, :] = jnp.where(two == 1, plane, field[k, 0:2, :])

        @pl.when(jnp.logical_not(has_high))
        def _():
            for k in range(fields):
                plane = jnp.broadcast_to(field[k, 9:10, :], (2, width))
                field[k, 10:12, :] = jnp.where(two == layers, plane, field[k, 10:12, :])

    def keep_edge(k, value):
        f_edge[k, 2:10, :] = value

    def keep_last(k, value):
        y_main[k] = value

    def emit_edges():
        first = lane < HALO
        outer = jnp.logical_or(first, lane >= width - HALO)
        for opening in range(0, fields, BATCH):
            made = []
            for k in range(opening, min(opening + BATCH, fields)):
                value = y_main[k]
                for layer in range(layers):
                    start = (layer + 1) * seg + HALO
                    moved = jnp.where(
                        first, shifted(value, -start), shifted(value, width - 4 * HALO - start)
                    )
                    made.append((k, layer, moved))
            for k, layer, moved in made:
                pltpu.store(out.at[k, 8 * layer : 8 * layer + 8, :], moved, mask=outer)

    link(e_edge)
    section(e_edge, 2, 8, e_edge, 2, 0.5, edge_rates, keep_edge, comps, nvars)
    link(f_edge)
    section(f_edge, 2, 8, e_edge, 2, 1.0, edge_rates, keep_last, comps, nvars)
    emit_edges()

    for copy in level:
        copy.wait_send()

    @pl.when(has_high)
    def _():
        for copy in up:
            copy.wait_send()

    @pl.when(has_low)
    def _():
        for copy in down:
            copy.wait_send()


def body(rows_total, blocks, state, inflow, blade_counts, modes):
    _, comps, nvars, depth, width = state.shape
    fields = comps * nvars
    seg, groups = packing(fields + comps, depth // 8, width)
    slots = width // (depth // 8 * seg) * (seg // HALO)
    corner_rows = -(-2 * groups // 8) * 8
    f32 = jnp.float32

    def buf(*shape):
        return pltpu.VMEM(shape, f32)

    tall = depth + 2 * PAD
    result = pl.pallas_call(
        functools.partial(kernel, rows_total, blocks, nvars),
        out_shape=jax.ShapeDtypeStruct((fields, depth, width), f32),
        in_specs=[
            pl.BlockSpec(memory_space=pltpu.HBM),
            pl.BlockSpec(memory_space=pltpu.HBM),
            pl.BlockSpec(memory_space=pltpu.HBM),
            pl.BlockSpec(memory_space=pltpu.HBM),
        ],
        out_specs=pl.BlockSpec(memory_space=pltpu.VMEM),
        scratch_shapes=[
            buf(fields, tall, width),
            buf(fields, 16, width),
            buf(fields, tall, width),
            buf(fields, 16, width),
            buf(fields, 16, width),
            buf(fields, 8, width),
            buf(comps, nvars, width),
            buf(comps, nvars, width),
            buf(2, groups, 8, width),
            buf(2, 2, corner_rows, width),
            buf(2, groups, 8, width),
            buf(fields, 8, width),
            buf(fields, 8, width),
            buf(2, corner_rows, width),
            buf(2, corner_rows, width),
            pltpu.SMEM(modes.shape, jnp.int32),
            pltpu.SMEM(blade_counts.shape, jnp.int32),
            pltpu.SemaphoreType.DMA((-(-fields // slots) + 3,)),
            pltpu.SemaphoreType.DMA((1,)),
            pltpu.SemaphoreType.DMA((8,)),
        ],
        compiler_params=pltpu.CompilerParams(
            collective_id=0, has_side_effects=True, vmem_limit_bytes=16 << 20
        ),
    )(
        *(
            pltpu.with_memory_space_constraint(value, pltpu.HBM)
            for value in (modes, blade_counts, state.reshape(fields, depth, width), inflow)
        )
    )
    return result.reshape(1, comps, nvars, depth, width)


def solution(mesh):
    placed = (P("row", None, None, None, "blk"), P(None, None, "blk"), P(), P())
    return jax.shard_map(
        functools.partial(body, mesh.shape["row"], mesh.shape["blk"]),
        mesh=mesh,
        in_specs=placed,
        out_specs=P("row", None, None, None, "blk"),
        check_vma=False,
    )
```

```python
import functools
import math

import jax
import jax.numpy as jnp
from jax import lax
from jax.experimental import pallas as pl
from jax.experimental.pallas import tpu as pltpu
from jax.sharding import PartitionSpec as P

DIFFUSE = 0.05
FOURTH_SMOOTH = 0.03
COURANT = 0.6
FREQ_SCALE = 0.02
MESH = pl.DeviceIdType.MESH
NEAR = DIFFUSE + 4.0 * FOURTH_SMOOTH
CENTER = -4.0 * DIFFUSE - 12.0 * FOURTH_SMOOTH
HALO = 4
PAD = 8
PIECES = 5
CHUNKS = 1


def packing(comps, nvars, layers, width):
    seg = width // (comps - 1)
    per = seg // HALO
    return seg, per, -(-layers * (nvars + 1) // per)


def shifted(value, by):
    by = by % value.shape[1]
    return value if by == 0 else pltpu.roll(value, by, 1)


def section(src, base, rows, start, start_base, weight, rates, emit, comps, nvars):
    def at(c, v, off):
        return src[c * nvars + v, base + off : base + off + rows, :]

    def opening(v):
        return start[v, start_base : start_base + rows, :]

    coef_up = (NEAR - 0.5) - 0.25 * jnp.tanh(at(0, 1, 1))
    coef_down = (NEAR + 0.5) + 0.25 * jnp.tanh(at(0, 1, -1))
    half_turn = 0.25 * jnp.tanh(at(0, 2, 0))
    coef_next = NEAR - shifted(half_turn, -1)
    coef_prev = NEAR + shifted(half_turn, 1)
    step = (weight * COURANT) / (
        1.0 + 0.5 * jnp.tanh(opening(1)) + jnp.abs(0.5 * jnp.tanh(opening(2)))
    )

    def one(c, v):
        here, up, down = at(c, v, 0), at(c, v, 1), at(c, v, -1)
        far = at(c, v, 2) + at(c, v, -2) + shifted(here, -2) + shifted(here, 2)
        total = (
            coef_up * up
            + coef_down * down
            + coef_next * shifted(here, -1)
            + coef_prev * shifted(here, 1)
            + CENTER * here
            - FOURTH_SMOOTH * far
        )
        return here, up, down, total

    def put(c, v, total):
        k = c * nvars + v
        emit(k, start[k, start_base : start_base + rows, :] + step * total)

    def per_var(v, carry):
        stress = None
        for n in range(1, comps // 2 + 1):
            real, real_up, real_down, real_total = one(2 * n - 1, v)
            imag, imag_up, imag_down, imag_total = one(2 * n, v)
            rate = rates[n - 1]
            put(2 * n - 1, v, real_total + rate * imag)
            put(2 * n, v, imag_total - rate * real)
            term = (
                at(2 * n - 1, 1, 1) * real_up
                + at(2 * n, 1, 1) * imag_up
                - at(2 * n - 1, 1, -1) * real_down
                - at(2 * n, 1, -1) * imag_down
            )
            stress = term if stress is None else stress + term
        _, _, _, total = one(0, v)
        put(0, v, total - 0.25 * stress)
        return carry

    lax.fori_loop(0, nvars, per_var, 0, unroll=True)


def strip_sections(works, nvars, seg):
    def lanes(work):
        return lax.broadcasted_iota(jnp.int32, (work["rows"], work["src"].shape[2]), 1)

    def at(work, g, off):
        first = work["base"] + off
        return work["src"][g, first : first + work["rows"], :]

    def opening(work, g):
        return work["start"][g, work["first"] : work["first"] + work["rows"], :]

    def spread(work, value, v, by=0):
        near = jnp.clip(lanes(work) % seg + by, 0, seg - 1)
        return jnp.take_along_axis(value, near + seg * v, axis=1)

    coefs = []
    for work in works:
        up = spread(work, at(work, nvars, 1), 1)
        down = spread(work, at(work, nvars, -1), 1)
        after = spread(work, at(work, nvars, 0), 2, 1)
        before = spread(work, at(work, nvars, 0), 2, -1)
        if work["step"] is None:
            axial = spread(work, opening(work, nvars), 1)
            turn = spread(work, opening(work, nvars), 2)
        else:
            axial = turn = None
        coefs.append((up, down, after, before, axial, turn))
    coefs = [
        (
            (NEAR - 0.5) - 0.25 * jnp.tanh(up),
            (NEAR + 0.5) + 0.25 * jnp.tanh(down),
            NEAR - 0.25 * jnp.tanh(after),
            NEAR + 0.25 * jnp.tanh(before),
            2.0 * work["step"]
            if axial is None
            else (0.5 * COURANT)
            / (1.0 + 0.5 * jnp.tanh(axial) + jnp.abs(0.5 * jnp.tanh(turn))),
        )
        for work, (up, down, after, before, axial, turn) in zip(works, coefs)
    ]
    stresses = []
    for work in works:
        one_up, one_down = at(work, 1, 1), at(work, 1, -1)
        terms = [one_up * at(work, v, 1) - one_down * at(work, v, -1) for v in range(nvars)]
        by = seg
        while by < work["src"].shape[2]:
            odd = (lanes(work) // by) % 2 == 1
            merged = []
            for i in range(0, len(terms), 2):
                a = terms[i]
                if i + 1 < len(terms):
                    b = terms[i + 1]
                    merged.append(jnp.where(odd, b, a) + shifted(jnp.where(odd, a, b), by))
                else:
                    merged.append(a + shifted(a, by))
            terms, by = merged, 2 * by
        stresses.append(terms[0])
    for g in range(nvars + 1):
        for work, stress, (coef_up, coef_down, coef_next, coef_prev, step) in zip(
            works, stresses, coefs
        ):
            here = at(work, g, 0)
            far = at(work, g, 2) + at(work, g, -2) + shifted(here, -2) + shifted(here, 2)
            total = (
                coef_up * at(work, g, 1)
                + coef_down * at(work, g, -1)
                + coef_next * shifted(here, -1)
                + coef_prev * shifted(here, 1)
                + CENTER * here
                - FOURTH_SMOOTH * far
            )
            if g == nvars:
                total = total - 0.25 * stress
            else:
                total = total + work["rate"] * shifted(here, here.shape[1] // 2)
            work["emit"](g, opening(work, g) + step * total)
    return [each[4] for each in coefs]


def kernel(
    rows_total,
    blocks,
    modes_in,
    counts_in,
    state,
    inflow,
    out,
    e_main,
    f_main,
    x_main,
    y_main,
    in_main,
    window,
    in_window,
    pack,
    corner,
    first_planes,
    last_planes,
    halo,
    low_halo,
    high_halo,
    low,
    high,
    low_window,
    high_window,
    e_side,
    f_side,
    x_side,
    y_side,
    result,
    modes,
    counts,
    local_sem,
    send_sem,
    recv_sem,
):
    fields, depth, width = state.shape
    comps, nvars, _ = inflow.shape
    harmonics = comps // 2
    layers = depth // 8
    seg, per, wires = packing(comps, nvars, layers, width)
    total_columns = width * blocks
    row = lax.axis_index("row")
    blk = lax.axis_index("blk")
    right = lax.rem(blk + 1, blocks)
    left = lax.rem(blk + blocks - 1, blocks)
    has_low = row > 0
    has_high = row < rows_total - 1

    barrier = pltpu.get_barrier_semaphore()

    def greet(r, b):
        pl.semaphore_signal(barrier, inc=1, device_id={"row": r, "blk": b}, device_id_type=MESH)

    greet(row, right)
    greet(row, left)

    @pl.when(has_high)
    def _():
        greet(row + 1, right)
        greet(row + 1, left)
        greet(row + 1, blk)

    @pl.when(has_low)
    def _():
        greet(row - 1, right)
        greet(row - 1, left)
        greet(row - 1, blk)

    def fetch(first, last, index):
        return pltpu.make_async_copy(
            state.at[first:last], e_main.at[first:last, PAD : PAD + depth, :], local_sem.at[index]
        )

    fetch_in = pltpu.make_async_copy(inflow, in_main, local_sem.at[CHUNKS])
    fetch_modes = pltpu.make_async_copy(modes_in, modes, local_sem.at[CHUNKS + 1])
    fetch_counts = pltpu.make_async_copy(counts_in, counts, local_sem.at[CHUNKS + 2])
    fetch_in.start()
    cuts = [comps * i // CHUNKS * nvars for i in range(CHUNKS + 1)]
    bounds = list(zip(cuts, cuts[1:]))
    for index, (opening, closing) in enumerate(bounds):
        for first in range(opening, closing, PIECES):
            fetch(first, min(first + PIECES, closing), index).start()
    fetch_modes.start()
    fetch_counts.start()

    shape = (8, width)
    sub = lax.broadcasted_iota(jnp.int32, shape, 0)
    lane = lax.broadcasted_iota(jnp.int32, shape, 1)
    part, near = lane // seg, lane % seg
    slot = near // HALO

    def seat(c, v):
        if c == 0:
            return nvars, v
        return v, (c - 1) // 2 + (0 if c % 2 else harmonics)

    fetch_in.wait()
    opened = None
    for c in range(1, comps):
        _, s = seat(c, 0)
        tile = shifted(in_main[c], seg * s + 2 * HALO)
        opened = tile if opened is None else jnp.where(part[0:nvars] == s, tile, opened)
    mean = None
    for v in range(nvars):
        tile = shifted(in_main[0, v : v + 1, :], seg * v + 2 * HALO)
        mean = tile if mean is None else jnp.where(part[0:1] == v, tile, mean)
    in_window[0:nvars, :] = opened
    in_window[nvars : nvars + 1, :] = mean
    for side in range(2):
        pack[side, wires, 0:nvars, :] = shifted(opened, -HALO * (2 - side))
        pack[side, wires, nvars : nvars + 1, :] = shifted(mean, -HALO * (2 - side))

    made = {}
    for index, (opening, closing) in enumerate(bounds):
        fetch(opening, closing, index).wait()
        for k in range(opening, closing):
            first_planes[k] = e_main[k, PAD : PAD + 4, :]
            last_planes[k] = e_main[k, PAD + depth - 4 : PAD + depth, :]
            g, s = seat(*divmod(k, nvars))
            for layer in range(layers):
                tile = shifted(
                    e_main[k, PAD + 8 * layer : PAD + 8 * layer + 8, :], seg * s + 2 * HALO
                )
                old = made.get((g, layer))
                made[g, layer] = tile if old is None else jnp.where(part == s, tile, old)
    targets = [(g, layer) for g in range(nvars + 1) for layer in range(layers)]
    for side in range(2):
        for wire in range(wires):
            value = None
            for i, target in enumerate(targets[wire * per : (wire + 1) * per]):
                moved = shifted(made[target], HALO * i - HALO * (2 - side))
                value = moved if value is None else jnp.where(slot == i, moved, value)
            pack[side, wire] = value
            corner[0, side, 2 * wire : 2 * wire + 2, :] = value[0:2]
            corner[1, side, 2 * wire : 2 * wire + 2, :] = value[6:8]
    for g, layer in targets:
        window[layer, g] = made[g, layer]

    greeters = 2 + 3 * has_low.astype(jnp.int32) + 3 * has_high.astype(jnp.int32)
    pl.semaphore_wait(barrier, greeters)

    def send(src, dst, index, r, b):
        return pltpu.make_async_remote_copy(
            src_ref=src,
            dst_ref=dst,
            send_sem=send_sem.at[0],
            recv_sem=recv_sem.at[index],
            device_id={"row": r, "blk": b},
            device_id_type=MESH,
        )

    level = [send(pack.at[1], halo.at[0], 0, row, right), send(pack.at[0], halo.at[1], 1, row, left)]
    more = 0 if rows_total == 2 else 4
    up = [
        send(corner.at[1, 1], low_halo.at[0], 2, row + 1, right),
        send(corner.at[1, 0], low_halo.at[1], 3, row + 1, left),
        send(last_planes, low, 4, row + 1, blk),
        send(window.at[layers - 1], low_window, 5, row + 1, blk),
    ]
    down = [
        send(corner.at[0, 1], high_halo.at[0], 2 + more, row - 1, right),
        send(corner.at[0, 0], high_halo.at[1], 3 + more, row - 1, left),
        send(first_planes, high, 4 + more, row - 1, blk),
        send(window.at[0], high_window, 5 + more, row - 1, blk),
    ]
    for copy in level:
        copy.start()

    @pl.when(has_high)
    def _():
        for copy in up:
            copy.start()

    @pl.when(has_low)
    def _():
        for copy in down:
            copy.start()

    fetch_modes.wait()
    fetch_counts.wait()
    sign = jnp.where((sub // 2) % 2 == 0, 1.0, -1.0).astype(jnp.float32)

    def mode_of(interface, n):
        value = jnp.int32(0)
        for i in range(rows_total - 1):
            value = value + jnp.where(interface == i, modes[i, n], 0)
        return value

    def count_of(wanted):
        value = jnp.int32(0)
        for i in range(rows_total):
            value = value + jnp.where(wanted == i, counts[i], 0)
        return value.astype(jnp.float32)

    def waves(mode, columns):
        product = mode * columns
        if total_columns & (total_columns - 1) == 0:
            turns = product & (total_columns - 1)
        else:
            turns = jnp.remainder(product, total_columns)
        angle = (2.0 * math.pi / total_columns) * turns.astype(jnp.float32)
        return jnp.cos(angle), jnp.sin(angle)

    def mode_at(n):
        return jnp.where(sub < 4, mode_of(row - 1, n), mode_of(row, n))

    tab_main = []
    for n in range(harmonics):
        cosine, sine = waves(mode_at(n), blk * width + lane)
        tab_main.append((cosine, sign * sine))

    order = part % harmonics
    lane_mode = jnp.zeros(shape, jnp.int32)
    for n in range(harmonics):
        lane_mode = jnp.where(order == n, mode_at(n), lane_mode)
    flip = jnp.where(part < harmonics, -1.0, 1.0).astype(jnp.float32)
    tab_side = []
    for side in range(2):
        column = near - 2 * HALO if side == 0 else near + width - 2 * HALO
        cosine, sine = waves(lane_mode, blk * width + column)
        tab_side.append((cosine, flip * sign * sine))

    own_rate = FREQ_SCALE * count_of(row)
    next_rate = jnp.where(sub < 4, FREQ_SCALE * count_of(row - 1), FREQ_SCALE * count_of(row + 1))
    own_rates = [own_rate * float(n) for n in range(1, harmonics + 1)]
    next_rates = [next_rate * float(n) for n in range(1, harmonics + 1)]
    times = -flip * (order + 1).astype(jnp.float32)
    side_rate = jnp.concatenate([times * own_rate] * layers, axis=0)
    side_next = times * next_rate

    @pl.when(has_low)
    def _():
        for copy in up[2:]:
            copy.wait_recv()
        x_main[:, 0:4, :] = low[...]

    @pl.when(jnp.logical_not(has_low))
    def _():
        x_main[:, 0:4, :] = jnp.zeros((fields, 4, width), jnp.float32)
        low_window[...] = jnp.zeros(low_window.shape, jnp.float32)

    @pl.when(has_high)
    def _():
        for copy in down[2:]:
            copy.wait_recv()
        x_main[:, 8:12, :] = high[...]

    @pl.when(jnp.logical_not(has_high))
    def _():
        x_main[:, 8:12, :] = jnp.zeros((fields, 4, width), jnp.float32)
        high_window[...] = jnp.zeros(high_window.shape, jnp.float32)

    def last_ends(field):
        @pl.when(jnp.logical_not(has_high))
        def _():
            for k in range(field.shape[0]):
                plane = field[k, PAD + depth - 1 : PAD + depth, :]
                field[k, PAD + depth : PAD + depth + 2, :] = jnp.broadcast_to(plane, (2, width))

    def ends(field):
        @pl.when(jnp.logical_not(has_low))
        def _():
            for c in range(comps):
                for v in range(nvars):
                    plane = in_main[c, v : v + 1, :]
                    field[c * nvars + v, PAD - 2 : PAD, :] = jnp.broadcast_to(plane, (2, width))

        last_ends(field)

    def turn(load, save, table):
        def per_var(v, carry):
            save(v, load(v))
            for n in range(harmonics):
                cosine, sine = table[n]
                real_at, imag_at = (2 * n + 1) * nvars + v, (2 * n + 2) * nvars + v
                real, imag = load(real_at), load(imag_at)
                save(real_at, real * cosine - imag * sine)
                save(imag_at, real * sine + imag * cosine)
            return carry

        lax.fori_loop(0, nvars, per_var, 0, unroll=True)

    def main():
        e, f, x, y = e_main, f_main, x_main, y_main
        x[:, 4:6, :] = e[:, PAD : PAD + 2, :]
        x[:, 6:8, :] = e[:, PAD + depth - 2 : PAD + depth, :]

        def save_first(k, value):
            e[k, PAD - 2 : PAD, :] = value[0:2]
            x[k, 4:8, :] = value[2:6]
            e[k, PAD + depth : PAD + depth + 2, :] = value[6:8]

        turn(lambda k: x[k, 2:10, :], save_first, tab_main)
        ends(e)

        def keep_y(k, value):
            y[k] = value

        def keep_f(k, value):
            f[k, PAD : PAD + depth, :] = value

        section(x, 2, 8, x, 2, 0.5, next_rates, keep_y, comps, nvars)
        section(e, PAD, depth, e, PAD, 0.5, own_rates, keep_f, comps, nvars)

        def save_second(k, value):
            f[k, PAD - 2 : PAD, :] = value[0:2]
            f[k, PAD + depth : PAD + depth + 2, :] = value[6:8]

        turn(lambda k: y[k], save_second, tab_main)
        ends(f)

        def emit(k, value):
            out[k] = value

        section(f, PAD, depth, e, PAD, 1.0, own_rates, emit, comps, nvars)

    def strip(side):
        level[side].wait_recv()
        if rows_total == 2:
            up[side].wait_recv()
        else:

            @pl.when(has_low)
            def _():
                up[side].wait_recv()

            @pl.when(has_high)
            def _():
                down[side].wait_recv()

        e, f, x, y = (ref.at[side] for ref in (e_side, f_side, x_side, y_side))
        spot = HALO * (1 + side)
        here = slot == 1 + side
        cosine, sine = tab_side[side]
        for wire in range(wires):
            value = halo[side, wire]
            for i, (g, layer) in enumerate(targets[wire * per : (wire + 1) * per]):
                tile = jnp.where(here, shifted(value, spot - HALO * i), window[layer, g])
                e[g, PAD + 8 * layer : PAD + 8 * layer + 8, :] = tile
                if layer == 0:
                    x[g, 4:6, :] = tile[0:2]
                if layer == layers - 1:
                    x[g, 6:8, :] = tile[6:8]
        for g in range(nvars + 1):
            x[g, 0:2, :] = low_window[g, 4:6, :]
            x[g, 10:12, :] = high_window[g, 2:4, :]
            for layer, corners, near_window, first, to in (
                (layers - 1, low_halo, low_window, 6, 2),
                (0, high_halo, high_window, 0, 8),
            ):
                at_wire, i = divmod(g * layers + layer, per)
                pair = shifted(corners[side, 2 * at_wire : 2 * at_wire + 2, :], spot - HALO * i)
                x[g, to : to + 2, :] = jnp.where(
                    here[0:2], pair, near_window[g, first : first + 2, :]
                )

        opened = jnp.where(here, shifted(halo[side, wires], spot), in_window[...])

        def link(field, g, value, last):
            low_end = jnp.broadcast_to(opened[g : g + 1], (2, width))
            high_end = jnp.broadcast_to(last, (2, width))
            field[g, PAD - 2 : PAD, :] = jnp.where(has_low, value[0:2], low_end)
            field[g, PAD + depth : PAD + depth + 2, :] = jnp.where(has_high, value[6:8], high_end)

        def turned(g, value):
            if g == nvars:
                return value
            return value * cosine + shifted(value, width // 2) * sine

        for g in range(nvars + 1):
            value = turned(g, x[g, 2:10, :])
            x[g, 4:8, :] = value[2:6]
            link(e, g, value, e[g, PAD + depth - 1 : PAD + depth, :])

        def keep_y(g, value):
            y[g] = value

        def keep_f(g, value):
            f[g, PAD : PAD + depth, :] = value

        def work(src, base, rows, first, rate, emit, step=None):
            return dict(
                src=src,
                base=base,
                rows=rows,
                start=x if src is x else e,
                first=first,
                step=step,
                rate=rate,
                emit=emit,
            )

        near_work = work(x, 2, 8, 2, side_next, keep_y)
        own_work = work(e, PAD, depth, PAD, side_rate, keep_f)
        _, own_step = strip_sections([near_work, own_work], nvars, seg)
        for g in range(nvars + 1):
            value = turned(g, y[g])
            link(f, g, value, f[g, PAD + depth - 1 : PAD + depth, :])

        kept = {}

        def keep(g, value):
            if side == 1:
                result[g] = value
            else:
                kept[g] = value

        strip_sections([work(f, PAD, depth, PAD, side_rate, keep, own_step)], nvars, seg)
        return kept

    def emit_edges(kept):
        outer = jnp.logical_or(lane < HALO, lane >= width - HALO)
        spots = sorted((seat(*divmod(k, nvars)), k) for k in range(fields))
        for g in range(nvars + 1):
            ready = []
            for layer in range(layers):
                rows = slice(8 * layer, 8 * layer + 8)
                both = jnp.where(near < 2 * HALO, result[g, rows, :], kept[g][rows])
                for (at_g, s), k in spots:
                    if at_g == g:
                        ready.append((k, rows, shifted(both, -seg * s - 2 * HALO)))
            for k, rows, value in ready:
                pltpu.store(out.at[k, rows, :], value, mask=outer)

    main()
    strip(1)
    emit_edges(strip(0))

    for copy in level:
        copy.wait_send()

    @pl.when(has_high)
    def _():
        for copy in up:
            copy.wait_send()

    @pl.when(has_low)
    def _():
        for copy in down:
            copy.wait_send()


def body(rows_total, blocks, state, inflow, blade_counts, modes):
    _, comps, nvars, depth, width = state.shape
    fields = comps * nvars
    layers = depth // 8
    kinds = nvars + 1
    _, _, wires = packing(comps, nvars, layers, width)
    corner_rows = -(-2 * wires // 8) * 8
    f32 = jnp.float32

    def buf(*shape):
        return pltpu.VMEM(shape, f32)

    tall = depth + 2 * PAD
    result = pl.pallas_call(
        functools.partial(kernel, rows_total, blocks),
        out_shape=jax.ShapeDtypeStruct((fields, depth, width), f32),
        in_specs=[pl.BlockSpec(memory_space=pltpu.HBM)] * 4,
        out_specs=pl.BlockSpec(memory_space=pltpu.VMEM),
        scratch_shapes=[
            buf(fields, tall, width),
            buf(fields, tall, width),
            buf(fields, 16, width),
            buf(fields, 8, width),
            buf(comps, nvars, width),
            buf(layers, kinds, 8, width),
            buf(8, width),
            buf(2, wires + 1, 8, width),
            buf(2, 2, corner_rows, width),
            buf(fields, 4, width),
            buf(fields, 4, width),
            buf(2, wires + 1, 8, width),
            buf(2, corner_rows, width),
            buf(2, corner_rows, width),
            buf(fields, 4, width),
            buf(fields, 4, width),
            buf(kinds, 8, width),
            buf(kinds, 8, width),
            buf(2, kinds, tall, width),
            buf(2, kinds, tall, width),
            buf(2, kinds, 16, width),
            buf(2, kinds, 8, width),
            buf(kinds, depth, width),
            pltpu.SMEM(modes.shape, jnp.int32),
            pltpu.SMEM(blade_counts.shape, jnp.int32),
            pltpu.SemaphoreType.DMA((CHUNKS + 3,)),
            pltpu.SemaphoreType.DMA((1,)),
            pltpu.SemaphoreType.DMA((6 if rows_total == 2 else 10,)),
        ],
        compiler_params=pltpu.CompilerParams(
            collective_id=0, has_side_effects=True, vmem_limit_bytes=16 << 20
        ),
    )(
        *(
            pltpu.with_memory_space_constraint(value, pltpu.HBM)
            for value in (modes, blade_counts, state.reshape(fields, depth, width), inflow)
        )
    )
    return result.reshape(1, comps, nvars, depth, width)


def solution(mesh):
    placed = (P("row", None, None, None, "blk"), P(None, None, "blk"), P(), P())
    return jax.shard_map(
        functools.partial(body, mesh.shape["row"], mesh.shape["blk"]),
        mesh=mesh,
        in_specs=placed,
        out_specs=P("row", None, None, None, "blk"),
        check_vma=False,
    )
```

```python
import functools
import math

import jax
import jax.numpy as jnp
from jax import lax
from jax.experimental import pallas as pl
from jax.experimental.pallas import tpu as pltpu
from jax.sharding import PartitionSpec as P

DIFFUSE = 0.05
FOURTH_SMOOTH = 0.03
COURANT = 0.6
FREQ_SCALE = 0.02
MESH = pl.DeviceIdType.MESH
NEAR = DIFFUSE + 4.0 * FOURTH_SMOOTH
CENTER = -4.0 * DIFFUSE - 12.0 * FOURTH_SMOOTH
HALO = 4
PAD = 8
PIECES = 5
CHUNKS = 2


def packing(comps, nvars, layers, width):
    seg = width // (comps - 1)
    per = seg // HALO
    return seg, per, -(-layers * (nvars + 1) // per)


def shifted(value, by):
    by = by % value.shape[1]
    return value if by == 0 else pltpu.roll(value, by, 1)


def section(src, base, rows, start, start_base, weight, rates, emit, comps, nvars):
    def at(c, v, off):
        return src[c * nvars + v, base + off : base + off + rows, :]

    def opening(v):
        return start[v, start_base : start_base + rows, :]

    coef_up = (NEAR - 0.5) - 0.25 * jnp.tanh(at(0, 1, 1))
    coef_down = (NEAR + 0.5) + 0.25 * jnp.tanh(at(0, 1, -1))
    half_turn = 0.25 * jnp.tanh(at(0, 2, 0))
    coef_next = NEAR - shifted(half_turn, -1)
    coef_prev = NEAR + shifted(half_turn, 1)
    step = (weight * COURANT) / (
        1.0 + 0.5 * jnp.tanh(opening(1)) + jnp.abs(0.5 * jnp.tanh(opening(2)))
    )

    def one(c, v):
        here, up, down = at(c, v, 0), at(c, v, 1), at(c, v, -1)
        far = at(c, v, 2) + at(c, v, -2) + shifted(here, -2) + shifted(here, 2)
        total = (
            coef_up * up
            + coef_down * down
            + coef_next * shifted(here, -1)
            + coef_prev * shifted(here, 1)
            + CENTER * here
            - FOURTH_SMOOTH * far
        )
        return here, up, down, total

    def put(c, v, total):
        k = c * nvars + v
        emit(k, start[k, start_base : start_base + rows, :] + step * total)

    def per_var(v, carry):
        stress = None
        for n in range(1, comps // 2 + 1):
            real, real_up, real_down, real_total = one(2 * n - 1, v)
            imag, imag_up, imag_down, imag_total = one(2 * n, v)
            rate = rates[n - 1]
            put(2 * n - 1, v, real_total + rate * imag)
            put(2 * n, v, imag_total - rate * real)
            term = (
                at(2 * n - 1, 1, 1) * real_up
                + at(2 * n, 1, 1) * imag_up
                - at(2 * n - 1, 1, -1) * real_down
                - at(2 * n, 1, -1) * imag_down
            )
            stress = term if stress is None else stress + term
        _, _, _, total = one(0, v)
        put(0, v, total - 0.25 * stress)
        return carry

    lax.fori_loop(0, nvars, per_var, 0, unroll=True)


def strip_sections(works, nvars, seg):
    def lanes(work):
        return lax.broadcasted_iota(jnp.int32, (work["rows"], work["src"].shape[2]), 1)

    def at(work, g, off):
        first = work["base"] + off
        return work["src"][g, first : first + work["rows"], :]

    def opening(work, g):
        return work["start"][g, work["first"] : work["first"] + work["rows"], :]

    def spread(work, value, v, by=0):
        near = jnp.clip(lanes(work) % seg + by, 0, seg - 1)
        return jnp.take_along_axis(value, near + seg * v, axis=1)

    coefs = []
    for work in works:
        up = spread(work, at(work, nvars, 1), 1)
        down = spread(work, at(work, nvars, -1), 1)
        after = spread(work, at(work, nvars, 0), 2, 1)
        before = spread(work, at(work, nvars, 0), 2, -1)
        if work["step"] is None:
            axial = spread(work, opening(work, nvars), 1)
            turn = spread(work, opening(work, nvars), 2)
        else:
            axial = turn = None
        coefs.append((up, down, after, before, axial, turn))
    coefs = [
        (
            (NEAR - 0.5) - 0.25 * jnp.tanh(up),
            (NEAR + 0.5) + 0.25 * jnp.tanh(down),
            NEAR - 0.25 * jnp.tanh(after),
            NEAR + 0.25 * jnp.tanh(before),
            2.0 * work["step"]
            if axial is None
            else (0.5 * COURANT)
            / (1.0 + 0.5 * jnp.tanh(axial) + jnp.abs(0.5 * jnp.tanh(turn))),
        )
        for work, (up, down, after, before, axial, turn) in zip(works, coefs)
    ]
    stresses = []
    for work in works:
        one_up, one_down = at(work, 1, 1), at(work, 1, -1)
        terms = [one_up * at(work, v, 1) - one_down * at(work, v, -1) for v in range(nvars)]
        by = seg
        while by < work["src"].shape[2]:
            odd = (lanes(work) // by) % 2 == 1
            merged = []
            for i in range(0, len(terms), 2):
                a = terms[i]
                if i + 1 < len(terms):
                    b = terms[i + 1]
                    merged.append(jnp.where(odd, b, a) + shifted(jnp.where(odd, a, b), by))
                else:
                    merged.append(a + shifted(a, by))
            terms, by = merged, 2 * by
        stresses.append(terms[0])
    for g in range(nvars + 1):
        for work, stress, (coef_up, coef_down, coef_next, coef_prev, step) in zip(
            works, stresses, coefs
        ):
            here = at(work, g, 0)
            far = at(work, g, 2) + at(work, g, -2) + shifted(here, -2) + shifted(here, 2)
            total = (
                coef_up * at(work, g, 1)
                + coef_down * at(work, g, -1)
                + coef_next * shifted(here, -1)
                + coef_prev * shifted(here, 1)
                + CENTER * here
                - FOURTH_SMOOTH * far
            )
            if g == nvars:
                total = total - 0.25 * stress
            else:
                total = total + work["rate"] * shifted(here, here.shape[1] // 2)
            work["emit"](g, opening(work, g) + step * total)
    return [each[4] for each in coefs]


def kernel(
    rows_total,
    blocks,
    modes_in,
    counts_in,
    state,
    inflow,
    out,
    e_main,
    f_main,
    x_main,
    y_main,
    g_main,
    in_main,
    window,
    in_window,
    pack,
    corner,
    first_planes,
    last_planes,
    halo,
    low_halo,
    high_halo,
    low,
    high,
    low_window,
    high_window,
    e_side,
    f_side,
    x_side,
    y_side,
    result,
    modes,
    counts,
    local_sem,
    send_sem,
    recv_sem,
):
    fields, depth, width = state.shape
    comps, nvars, _ = inflow.shape
    harmonics = comps // 2
    layers = depth // 8
    seg, per, wires = packing(comps, nvars, layers, width)
    total_columns = width * blocks
    row = lax.axis_index("row")
    blk = lax.axis_index("blk")
    right = lax.rem(blk + 1, blocks)
    left = lax.rem(blk + blocks - 1, blocks)
    has_low = row > 0
    has_high = row < rows_total - 1

    barrier = pltpu.get_barrier_semaphore()

    def greet(r, b):
        pl.semaphore_signal(barrier, inc=1, device_id={"row": r, "blk": b}, device_id_type=MESH)

    greet(row, right)
    greet(row, left)

    @pl.when(has_high)
    def _():
        greet(row + 1, right)
        greet(row + 1, left)
        greet(row + 1, blk)

    @pl.when(has_low)
    def _():
        greet(row - 1, right)
        greet(row - 1, left)
        greet(row - 1, blk)

    def fetch(first, last, index):
        return pltpu.make_async_copy(
            state.at[first:last], e_main.at[first:last, PAD : PAD + depth, :], local_sem.at[index]
        )

    fetch_in = pltpu.make_async_copy(inflow, in_main, local_sem.at[CHUNKS])
    fetch_modes = pltpu.make_async_copy(modes_in, modes, local_sem.at[CHUNKS + 1])
    fetch_counts = pltpu.make_async_copy(counts_in, counts, local_sem.at[CHUNKS + 2])
    fetch_in.start()
    cuts = [comps * i // CHUNKS * nvars for i in range(CHUNKS + 1)]
    bounds = list(zip(cuts, cuts[1:]))
    for index, (opening, closing) in enumerate(bounds):
        for first in range(opening, closing, PIECES):
            fetch(first, min(first + PIECES, closing), index).start()
    fetch_modes.start()
    fetch_counts.start()

    shape = (8, width)
    sub = lax.broadcasted_iota(jnp.int32, shape, 0)
    lane = lax.broadcasted_iota(jnp.int32, shape, 1)
    part, near = lane // seg, lane % seg
    slot = near // HALO

    def seat(c, v):
        if c == 0:
            return nvars, v
        return v, (c - 1) // 2 + (0 if c % 2 else harmonics)

    fetch_in.wait()
    opened = None
    for c in range(1, comps):
        _, s = seat(c, 0)
        tile = shifted(in_main[c], seg * s + 2 * HALO)
        opened = tile if opened is None else jnp.where(part[0:nvars] == s, tile, opened)
    mean = None
    for v in range(nvars):
        tile = shifted(in_main[0, v : v + 1, :], seg * v + 2 * HALO)
        mean = tile if mean is None else jnp.where(part[0:1] == v, tile, mean)
    in_window[0:nvars, :] = opened
    in_window[nvars : nvars + 1, :] = mean
    for side in range(2):
        pack[side, wires, 0:nvars, :] = shifted(opened, -HALO * (2 - side))
        pack[side, wires, nvars : nvars + 1, :] = shifted(mean, -HALO * (2 - side))

    made = {}
    for index, (opening, closing) in enumerate(bounds):
        fetch(opening, closing, index).wait()
        for k in range(opening, closing):
            first_planes[k] = e_main[k, PAD : PAD + 4, :]
            last_planes[k] = e_main[k, PAD + depth - 4 : PAD + depth, :]
            g, s = seat(*divmod(k, nvars))
            for layer in range(layers):
                tile = shifted(
                    e_main[k, PAD + 8 * layer : PAD + 8 * layer + 8, :], seg * s + 2 * HALO
                )
                old = made.get((g, layer))
                made[g, layer] = tile if old is None else jnp.where(part == s, tile, old)
    targets = [(g, layer) for g in range(nvars + 1) for layer in range(layers)]
    def pack_side(side):
        for wire in range(wires):
            value = None
            for i, target in enumerate(targets[wire * per : (wire + 1) * per]):
                moved = shifted(made[target], HALO * i - HALO * (2 - side))
                value = moved if value is None else jnp.where(slot == i, moved, value)
            pack[side, wire] = value
            corner[0, side, 2 * wire : 2 * wire + 2, :] = value[0:2]
            corner[1, side, 2 * wire : 2 * wire + 2, :] = value[6:8]

    pack_side(1)

    def count_of(wanted):
        value = jnp.int32(0)
        for i in range(rows_total):
            value = value + jnp.where(wanted == i, counts[i], 0)
        return value.astype(jnp.float32)

    def rates_of(rate):
        return [rate * float(n) for n in range(1, harmonics + 1)]

    def inner():
        fetch_modes.wait()
        fetch_counts.wait()
        own_rates = rates_of(FREQ_SCALE * count_of(row))
        g_main[:, 2:6, :] = e_main[:, PAD : PAD + 4, :]
        g_main[:, 6:10, :] = e_main[:, PAD + depth - 4 : PAD + depth, :]

        def keep(k, value):
            f_main[k, PAD : PAD + depth, :] = value

        section(e_main, PAD, depth, e_main, PAD, 0.5, own_rates, keep, comps, nvars)

    @pl.when(blk == 0)
    def _():
        inner()

    greeters = 2 + 3 * has_low.astype(jnp.int32) + 3 * has_high.astype(jnp.int32)
    pl.semaphore_wait(barrier, greeters)

    def send(src, dst, index, r, b):
        return pltpu.make_async_remote_copy(
            src_ref=src,
            dst_ref=dst,
            send_sem=send_sem.at[0],
            recv_sem=recv_sem.at[index],
            device_id={"row": r, "blk": b},
            device_id_type=MESH,
        )

    level = [send(pack.at[1], halo.at[0], 0, row, right), send(pack.at[0], halo.at[1], 1, row, left)]
    more = 0 if rows_total == 2 else 4
    up = [
        send(corner.at[1, 1], low_halo.at[0], 2, row + 1, right),
        send(corner.at[1, 0], low_halo.at[1], 3, row + 1, left),
        send(last_planes, low, 4, row + 1, blk),
        send(window.at[layers - 1], low_window, 5, row + 1, blk),
    ]
    down = [
        send(corner.at[0, 1], high_halo.at[0], 2 + more, row - 1, right),
        send(corner.at[0, 0], high_halo.at[1], 3 + more, row - 1, left),
        send(first_planes, high, 4 + more, row - 1, blk),
        send(window.at[0], high_window, 5 + more, row - 1, blk),
    ]
    level[0].start()
    pack_side(0)
    for g, layer in targets:
        window[layer, g] = made[g, layer]
    level[1].start()

    @pl.when(has_high)
    def _():
        for copy in up:
            copy.start()

    @pl.when(has_low)
    def _():
        for copy in down:
            copy.start()

    @pl.when(blk != 0)
    def _():
        inner()

    sign = jnp.where((sub // 2) % 2 == 0, 1.0, -1.0).astype(jnp.float32)

    def mode_of(interface, n):
        value = jnp.int32(0)
        for i in range(rows_total - 1):
            value = value + jnp.where(interface == i, modes[i, n], 0)
        return value

    def waves(mode, columns):
        product = mode * columns
        if total_columns & (total_columns - 1) == 0:
            turns = product & (total_columns - 1)
        else:
            turns = jnp.remainder(product, total_columns)
        angle = (2.0 * math.pi / total_columns) * turns.astype(jnp.float32)
        return jnp.cos(angle), jnp.sin(angle)

    def mode_at(n):
        return jnp.where(sub < 4, mode_of(row - 1, n), mode_of(row, n))

    tab_main = []
    for n in range(harmonics):
        cosine, sine = waves(mode_at(n), blk * width + lane)
        tab_main.append((cosine, sign * sine))

    order = part % harmonics
    lane_mode = jnp.zeros(shape, jnp.int32)
    for n in range(harmonics):
        lane_mode = jnp.where(order == n, mode_at(n), lane_mode)
    flip = jnp.where(part < harmonics, -1.0, 1.0).astype(jnp.float32)
    tab_side = []
    for side in range(2):
        column = near - 2 * HALO if side == 0 else near + width - 2 * HALO
        cosine, sine = waves(lane_mode, blk * width + column)
        tab_side.append((cosine, flip * sign * sine))

    next_rate = jnp.where(sub < 4, FREQ_SCALE * count_of(row - 1), FREQ_SCALE * count_of(row + 1))
    own_rate = FREQ_SCALE * count_of(row)
    own_rates, next_rates = rates_of(own_rate), rates_of(next_rate)
    times = -flip * (order + 1).astype(jnp.float32)
    side_rate = jnp.concatenate([times * own_rate] * layers, axis=0)
    side_next = times * next_rate

    @pl.when(has_low)
    def _():
        for copy in up[2:]:
            copy.wait_recv()
        x_main[:, 0:4, :] = low[...]

    @pl.when(jnp.logical_not(has_low))
    def _():
        x_main[:, 0:4, :] = jnp.zeros((fields, 4, width), jnp.float32)
        low_window[...] = jnp.zeros(low_window.shape, jnp.float32)

    @pl.when(has_high)
    def _():
        for copy in down[2:]:
            copy.wait_recv()
        x_main[:, 8:12, :] = high[...]

    @pl.when(jnp.logical_not(has_high))
    def _():
        x_main[:, 8:12, :] = jnp.zeros((fields, 4, width), jnp.float32)
        high_window[...] = jnp.zeros(high_window.shape, jnp.float32)

    def ends(field, low_at, high_at):
        @pl.when(jnp.logical_not(has_low))
        def _():
            for c in range(comps):
                for v in range(nvars):
                    plane = in_main[c, v : v + 1, :]
                    field[c * nvars + v, low_at : low_at + 2, :] = jnp.broadcast_to(
                        plane, (2, width)
                    )

        @pl.when(jnp.logical_not(has_high))
        def _():
            for k in range(fields):
                plane = field[k, high_at - 1 : high_at, :]
                field[k, high_at : high_at + 2, :] = jnp.broadcast_to(plane, (2, width))

    def turn(load, save, table):
        def per_var(v, carry):
            save(v, load(v))
            for n in range(harmonics):
                cosine, sine = table[n]
                real_at, imag_at = (2 * n + 1) * nvars + v, (2 * n + 2) * nvars + v
                real, imag = load(real_at), load(imag_at)
                save(real_at, real * cosine - imag * sine)
                save(imag_at, real * sine + imag * cosine)
            return carry

        lax.fori_loop(0, nvars, per_var, 0, unroll=True)

    def main():
        e, f, g, x, y = e_main, f_main, g_main, x_main, y_main
        x[:, 4:6, :] = e[:, PAD : PAD + 2, :]
        x[:, 6:8, :] = e[:, PAD + depth - 2 : PAD + depth, :]

        def save_first(k, value):
            g[k, 0:2, :] = value[0:2]
            x[k, 4:8, :] = value[2:6]
            g[k, 10:12, :] = value[6:8]

        turn(lambda k: x[k, 2:10, :], save_first, tab_main)
        ends(g, 0, 10)

        def keep_y(k, value):
            y[k] = value

        def keep_outer(k, value):
            f[k, PAD : PAD + 2, :] = value[0:2]
            f[k, PAD + depth - 2 : PAD + depth, :] = value[6:8]

        section(x, 2, 8, x, 2, 0.5, next_rates, keep_y, comps, nvars)
        section(g, 2, 8, g, 2, 0.5, own_rates, keep_outer, comps, nvars)

        def save_second(k, value):
            f[k, PAD - 2 : PAD, :] = value[0:2]
            f[k, PAD + depth : PAD + depth + 2, :] = value[6:8]

        turn(lambda k: y[k], save_second, tab_main)
        ends(f, PAD - 2, PAD + depth)

        def emit(k, value):
            out[k] = value

        section(f, PAD, depth, e, PAD, 1.0, own_rates, emit, comps, nvars)

    def strip(side):
        level[side].wait_recv()
        if rows_total == 2:
            up[side].wait_recv()
        else:

            @pl.when(has_low)
            def _():
                up[side].wait_recv()

            @pl.when(has_high)
            def _():
                down[side].wait_recv()

        e, f, x, y = (ref.at[side] for ref in (e_side, f_side, x_side, y_side))
        spot = HALO * (1 + side)
        here = slot == 1 + side
        cosine, sine = tab_side[side]
        for wire in range(wires):
            value = halo[side, wire]
            for i, (g, layer) in enumerate(targets[wire * per : (wire + 1) * per]):
                tile = jnp.where(here, shifted(value, spot - HALO * i), window[layer, g])
                e[g, PAD + 8 * layer : PAD + 8 * layer + 8, :] = tile
                if layer == 0:
                    x[g, 4:6, :] = tile[0:2]
                if layer == layers - 1:
                    x[g, 6:8, :] = tile[6:8]
        for g in range(nvars + 1):
            x[g, 0:2, :] = low_window[g, 4:6, :]
            x[g, 10:12, :] = high_window[g, 2:4, :]
            for layer, corners, near_window, first, to in (
                (layers - 1, low_halo, low_window, 6, 2),
                (0, high_halo, high_window, 0, 8),
            ):
                at_wire, i = divmod(g * layers + layer, per)
                pair = shifted(corners[side, 2 * at_wire : 2 * at_wire + 2, :], spot - HALO * i)
                x[g, to : to + 2, :] = jnp.where(
                    here[0:2], pair, near_window[g, first : first + 2, :]
                )

        opened = jnp.where(here, shifted(halo[side, wires], spot), in_window[...])

        def link(field, g, value, last):
            low_end = jnp.broadcast_to(opened[g : g + 1], (2, width))
            high_end = jnp.broadcast_to(last, (2, width))
            field[g, PAD - 2 : PAD, :] = jnp.where(has_low, value[0:2], low_end)
            field[g, PAD + depth : PAD + depth + 2, :] = jnp.where(has_high, value[6:8], high_end)

        def turned(g, value):
            if g == nvars:
                return value
            return value * cosine + shifted(value, width // 2) * sine

        for g in range(nvars + 1):
            value = turned(g, x[g, 2:10, :])
            x[g, 4:8, :] = value[2:6]
            link(e, g, value, e[g, PAD + depth - 1 : PAD + depth, :])

        def keep_y(g, value):
            y[g] = value

        def keep_f(g, value):
            f[g, PAD : PAD + depth, :] = value

        def work(src, base, rows, first, rate, emit, step=None):
            return dict(
                src=src,
                base=base,
                rows=rows,
                start=x if src is x else e,
                first=first,
                step=step,
                rate=rate,
                emit=emit,
            )

        near_work = work(x, 2, 8, 2, side_next, keep_y)
        own_work = work(e, PAD, depth, PAD, side_rate, keep_f)
        _, own_step = strip_sections([near_work, own_work], nvars, seg)
        for g in range(nvars + 1):
            value = turned(g, y[g])
            link(f, g, value, f[g, PAD + depth - 1 : PAD + depth, :])

        kept = {}

        def keep(g, value):
            if side == 1:
                result[g] = value
            else:
                kept[g] = value

        strip_sections([work(f, PAD, depth, PAD, side_rate, keep, own_step)], nvars, seg)
        return kept

    def emit_edges(kept):
        outer = jnp.logical_or(lane < HALO, lane >= width - HALO)
        spots = sorted((seat(*divmod(k, nvars)), k) for k in range(fields))
        for g in range(nvars + 1):
            ready = []
            for layer in range(layers):
                rows = slice(8 * layer, 8 * layer + 8)
                both = jnp.where(near < 2 * HALO, result[g, rows, :], kept[g][rows])
                for (at_g, s), k in spots:
                    if at_g == g:
                        ready.append((k, rows, shifted(both, -seg * s - 2 * HALO)))
            for k, rows, value in ready:
                pltpu.store(out.at[k, rows, :], value, mask=outer)

    main()
    strip(1)
    emit_edges(strip(0))

    for copy in level:
        copy.wait_send()

    @pl.when(has_high)
    def _():
        for copy in up:
            copy.wait_send()

    @pl.when(has_low)
    def _():
        for copy in down:
            copy.wait_send()


def body(rows_total, blocks, state, inflow, blade_counts, modes):
    _, comps, nvars, depth, width = state.shape
    fields = comps * nvars
    layers = depth // 8
    kinds = nvars + 1
    _, _, wires = packing(comps, nvars, layers, width)
    corner_rows = -(-2 * wires // 8) * 8
    f32 = jnp.float32

    def buf(*shape):
        return pltpu.VMEM(shape, f32)

    tall = depth + 2 * PAD
    result = pl.pallas_call(
        functools.partial(kernel, rows_total, blocks),
        out_shape=jax.ShapeDtypeStruct((fields, depth, width), f32),
        in_specs=[pl.BlockSpec(memory_space=pltpu.HBM)] * 4,
        out_specs=pl.BlockSpec(memory_space=pltpu.VMEM),
        scratch_shapes=[
            buf(fields, tall, width),
            buf(fields, tall, width),
            buf(fields, 16, width),
            buf(fields, 8, width),
            buf(fields, 16, width),
            buf(comps, nvars, width),
            buf(layers, kinds, 8, width),
            buf(8, width),
            buf(2, wires + 1, 8, width),
            buf(2, 2, corner_rows, width),
            buf(fields, 4, width),
            buf(fields, 4, width),
            buf(2, wires + 1, 8, width),
            buf(2, corner_rows, width),
            buf(2, corner_rows, width),
            buf(fields, 4, width),
            buf(fields, 4, width),
            buf(kinds, 8, width),
            buf(kinds, 8, width),
            buf(2, kinds, tall, width),
            buf(2, kinds, tall, width),
            buf(2, kinds, 16, width),
            buf(2, kinds, 8, width),
            buf(kinds, depth, width),
            pltpu.SMEM(modes.shape, jnp.int32),
            pltpu.SMEM(blade_counts.shape, jnp.int32),
            pltpu.SemaphoreType.DMA((CHUNKS + 3,)),
            pltpu.SemaphoreType.DMA((1,)),
            pltpu.SemaphoreType.DMA((6 if rows_total == 2 else 10,)),
        ],
        compiler_params=pltpu.CompilerParams(
            collective_id=0, has_side_effects=True, vmem_limit_bytes=16 << 20
        ),
    )(
        *(
            pltpu.with_memory_space_constraint(value, pltpu.HBM)
            for value in (modes, blade_counts, state.reshape(fields, depth, width), inflow)
        )
    )
    return result.reshape(1, comps, nvars, depth, width)


def solution(mesh):
    placed = (P("row", None, None, None, "blk"), P(None, None, "blk"), P(), P())
    return jax.shard_map(
        functools.partial(body, mesh.shape["row"], mesh.shape["blk"]),
        mesh=mesh,
        in_specs=placed,
        out_specs=P("row", None, None, None, "blk"),
        check_vma=False,
    )
```
